256 devices in a mesh: dp: 16 (over y, x), seq: 16 (over z, core).
Axes of the slice: x: 4, y: 4, z: 8, core: 2. Of those that a mesh axis runs over, the one named last changes fastest.
Arguments:
- query_states: bfloat16 [16, 2048, 5120], P('dp', 'seq'), may hold values from -36 to 36
- key_states: bfloat16 [16, 2048, 1024], P('dp', 'seq'), may hold values from -3 to 3
- value_states: bfloat16 [16, 2048, 1024], P('dp', 'seq'), may hold values from -6 to 6
- output_grad: bfloat16 [16, 2048, 5120], P('dp', 'seq'), may hold values from -6 to 6
- layer_input: bfloat16 [16, 2048, 4096], P('dp', 'seq'), may hold values from -6 to 6
- head_counts: int32 [8], replicated, may hold values from 1 to 8, 40 in all
Outputs:
- query_grad: bfloat16 [16, 2048, 5120], P('dp', 'seq')
- key_grad: bfloat16 [16, 2048, 1024], P('dp', 'seq')
- weight_grad: float32 [4096, 512], P(('dp', 'seq'))
The draws below stay inside these ranges and needn't reach their ends.
Inputs may be any that keep to these rules, and one draw needn't show every extreme that they name: `head_counts`: kept query heads of each of the 8 groups; they sum to 40, and some group keeps all 8.
All inputs are finite; a program needn't handle non-finite values.
Results may differ from the reference program's by a relative error of at most 0.0085.
Values may be sent and summed in bfloat16 or wider, within the bound.
A program may use at most 128 MiB of HBM per device.

```python
import math
import jax
import jax.numpy as jnp
import numpy as np
from jax import lax

HD = 128
KVG = 8
QPG = 8
HKEPT = 40
DWIN = 4096
VGW = 4
SEQ_LEN = 2048
BATCH = 16
QW = 5120
KVW = 1024


def draw_key_states(key, part):
    base = jnp.clip(jax.random.normal(jax.random.fold_in(key, 11), (BATCH, SEQ_LEN, KVW)), -3.0, 3.0)
    return base.astype(jnp.bfloat16)


def draw_query_states(key, part):
    base = jnp.clip(jax.random.normal(jax.random.fold_in(key, 21), (BATCH, SEQ_LEN, QW)), -3.0, 3.0)
    return base.astype(jnp.bfloat16)


def raised(values, rng, source, target, blocks, factor):
    owner, partner = [(jnp.arange(values.shape[position]) // (values.shape[position] // blocks)).reshape([-1 if axis == position else 1 for axis in range(values.ndim)]) for position in (source, target)]
    chosen = jax.random.permutation(rng, blocks)[partner]
    strong = (owner == chosen) | (owner == (partner + blocks // 2) % blocks)
    return jnp.where(strong, factor * values, values)


def shard_levels(key, shape, split, smallest, high):
    loudness, own = 1.0, jax.random.fold_in(key, 6)
    for dim, blocks in split:
        draws = jnp.exp(jax.random.uniform(jax.random.fold_in(own, dim), (blocks,), jnp.float32, smallest / len(split), high / len(split)))
        loudness = loudness * jnp.repeat(draws, shape[dim] // blocks).reshape([-1 if axis == dim else 1 for axis in range(len(shape))])
    return loudness


def split_up(amount, total, limit, lean):
    portions = [(1 << 20) // math.isqrt(standing ** lean) + 1 for standing in range(2, amount + 1)]
    spare, holding = total - limit - (amount - 1), [1] * (amount - 1)
    while spare > 0:
        movable = [i for i in range(amount - 1) if holding[i] < limit]
        mass, budget = sum([portions[i] for i in movable]), spare
        for i in movable:
            extra = min(limit - holding[i], max(1, budget * portions[i] // mass), spare)
            holding[i] = holding[i] + extra
            spare = spare - extra
    return np.array([limit] + holding)


def ragged_sizes(own_key, amount, total, bound, lean):
    if amount == 2:
        one = jax.random.randint(own_key, (), max(1, total - bound), min(bound, total - 1) + 1)
        return jnp.stack([one, total - one])
    lengths = jnp.asarray(split_up(amount, total, bound, lean), jnp.int32)
    pairs = (amount - 1) // 2
    giver, sink = lengths[1:1 + 2 * pairs:2], lengths[2:2 + 2 * pairs:2]
    margin = jnp.minimum(giver - 1, bound - sink)
    shifted = jax.random.randint(jax.random.fold_in(own_key, 1), (pairs,), 0, 1 << 20) % (margin + 1)
    lengths = lengths.at[1:1 + 2 * pairs:2].set(giver - shifted).at[2:2 + 2 * pairs:2].set(sink + shifted)
    return lengths[jax.random.permutation(jax.random.fold_in(own_key, 2), amount)]


def noise(key, extent, deviation, bound, pieces=(), kind=jnp.bfloat16):
    loudness = shard_levels(key, extent, pieces, -0.22, 0.18) if pieces else 1.0
    array = jax.random.normal(key, extent, jnp.float32) * deviation * loudness
    return jnp.minimum(jnp.maximum(array, -bound), bound).astype(kind)


def bell_draw_with(stream_key, shape, spread, most, shards, heavy, kind=jnp.bfloat16):
    array = spread * jax.random.normal(stream_key, shape, jnp.float32)
    if shards:
        array = array * shard_levels(stream_key, shape, shards, -0.22, 0.18)
    return jnp.clip(raised(array, jax.random.fold_in(stream_key, 3), *heavy), -most, most).astype(kind)


def setup_inputs(seed: int = 0) -> dict:
    key_list = jax.random.split(jax.random.key(seed), 7)
    return {
        "query_states": draw_query_states(jax.random.fold_in(key_list[6], 71), 0),
        "key_states": draw_key_states(jax.random.fold_in(key_list[6], 71), 0),
        "value_states": noise(key_list[2], (BATCH, SEQ_LEN, KVW), 1.0, 6.0, ((0, 16), (1, 16))),
        "output_grad": noise(key_list[3], (BATCH, SEQ_LEN, QW), 1.0, 6.0, ((0, 16), (1, 16))),
        "layer_input": bell_draw_with(key_list[4], (BATCH, SEQ_LEN, DWIN), 1.0, 6.0, ((0, 16), (1, 16)), (1, 2, 16, 2.0)),
        "head_counts": ragged_sizes(key_list[5], KVG, HKEPT, QPG, 1).astype(jnp.int32),
    }


masked_score = -1e+30

def head_backward(queries, key_rows, value_rows, grad_rows):
    sequence = queries.shape[0]
    scaling = 1.0 / math.sqrt(queries.shape[1])
    scores = jnp.dot(queries, key_rows.T, preferred_element_type=jnp.float32) * scaling
    row_position = lax.broadcasted_iota(jnp.int32, (sequence, sequence), 0)
    column_position = lax.broadcasted_iota(jnp.int32, (sequence, sequence), 1)
    scores = jnp.where(column_position <= row_position, scores, masked_score)
    top_score = lax.optimization_barrier(jnp.max(scores, axis=1, keepdims=True))
    weights = jnp.exp(scores - top_score)
    softmax_rows = weights / lax.optimization_barrier(jnp.sum(weights, axis=1, keepdims=True))
    softmax_half = softmax_rows.astype(jnp.bfloat16)
    grad_weights = jnp.dot(grad_rows, value_rows.T, preferred_element_type=jnp.float32)
    row_terms = lax.optimization_barrier(jnp.sum(softmax_rows * grad_weights, axis=1, keepdims=True))
    grad_scores = (softmax_rows * (grad_weights - row_terms) * scaling).astype(jnp.bfloat16)
    grad_query = jnp.dot(grad_scores, key_rows, preferred_element_type=jnp.float32).astype(jnp.bfloat16)
    grad_key = jnp.dot(grad_scores.T, queries, preferred_element_type=jnp.float32).astype(jnp.bfloat16)
    grad_value = jnp.dot(softmax_half.T, grad_rows, preferred_element_type=jnp.float32).astype(jnp.bfloat16)
    return (grad_query, grad_key, grad_value)

def apply_head(item):
    return head_backward(item[0], item[1], item[2], item[3])

def one_sequence(group_of, group_hot, states):
    query_rows = states[0]
    sequence = query_rows.shape[0]
    query_heads = query_rows.reshape(sequence, HKEPT, HD).transpose(1, 0, 2)
    key_heads = states[1].reshape(sequence, KVG, HD)[:, group_of, :].transpose(1, 0, 2)
    value_heads = states[2].reshape(sequence, KVG, HD)[:, group_of, :].transpose(1, 0, 2)
    grad_heads = states[3].reshape(sequence, HKEPT, HD).transpose(1, 0, 2)
    results = lax.map(apply_head, (query_heads, key_heads, value_heads, grad_heads))
    query_grad = results[0].transpose(1, 0, 2).reshape(sequence, HKEPT * HD)
    key_grad = jnp.einsum('hsc,hg->sgc', results[1].astype(jnp.float32), group_hot)
    value_grad = jnp.einsum('hsc,hg->sgc', results[2].astype(jnp.float32), group_hot)
    key_grad = key_grad.astype(jnp.bfloat16).reshape(sequence, KVG * HD)
    value_grad = value_grad.astype(jnp.bfloat16).reshape(sequence, KVG * HD)
    return (query_grad, key_grad, value_grad)

def reference(query_states, key_states, value_states, output_grad, layer_input, head_counts):
    head_index = jnp.arange(HKEPT, dtype=jnp.int32)
    group_ends = jnp.cumsum(head_counts).astype(jnp.int32)
    group_of = lax.optimization_barrier(jnp.sum((group_ends[None, :] <= head_index[:, None]).astype(jnp.int32), axis=1)).astype(jnp.int32)
    group_hot = (group_of[:, None] == jnp.arange(KVG, dtype=jnp.int32)[None, :]).astype(jnp.float32)

    def per_sequence(states):
        return one_sequence(group_of, group_hot, states)
    query_grad, key_grad, value_grad = lax.map(per_sequence, (query_states, key_states, value_states, output_grad))
    layer_rows = layer_input.reshape(-1, DWIN)
    value_window = value_grad.reshape(-1, KVG * HD)[:, :VGW * HD]
    weight_grad = jnp.dot(layer_rows.T, value_window, preferred_element_type=jnp.float32)
    return (query_grad, key_grad, weight_grad)
```

```python
import functools
import math

import jax
import jax.numpy as jnp
from jax import lax
from jax.experimental import pallas as pl
from jax.experimental.pallas import tpu as pltpu
from jax.sharding import PartitionSpec as P

HD = 128
KVG = 8
HKEPT = 40
VGW = 4
CHUNK = 512

masked_score = -1e30
NT = (((1,), (1,)), ((), ()))
NN = (((1,), (0,)), ((), ()))


def matmul(a, b, dims):
    return lax.dot_general(a, b, dims, preferred_element_type=jnp.float32)


def fold_rows(x, op):
    rows, columns = x.shape
    return op(x.reshape(rows // 8, 8, columns), axis=0)


def attention_kernel(
    info, q_ref, do_ref, kv_ref, dq_ref, dkv_ref,
    qs, dos, s_scr, dp_scr, acc, kt_scr,
):
    group = pl.program_id(0)
    block = info[2 * KVG]
    first_head = info[group]
    head_count = info[KVG + group]
    tokens = q_ref.shape[0]
    scaling = 1.0 / math.sqrt(HD)
    to_exp2 = scaling * math.log2(math.e)
    last = (block * tokens) // CHUNK
    row_base = block * tokens

    def rows_at(c):
        return pl.ds(pl.multiple_of(c * CHUNK, CHUNK), CHUNK)

    def prepare(c, _):
        rows = rows_at(c)
        kt_scr[:, rows] = kv_ref[rows, :HD].T
        acc[rows, :] = jnp.zeros((CHUNK, 2 * HD), jnp.float32)
        return 0

    lax.fori_loop(0, last + 1, prepare, 0)

    def run_heads(head, count):
        width = count * tokens
        for i in range(count):
            columns = pl.ds(pl.multiple_of((head + i) * HD, HD), HD)
            qs[i * tokens:(i + 1) * tokens, :] = q_ref[:, columns]
            dos[i * tokens:(i + 1) * tokens, :] = do_ref[:, columns]
        q = qs[:width, :]
        do = dos[:width, :]

        def scores(c, top, masked):
            rows = rows_at(c)
            s = matmul(kv_ref[rows, :HD], q, NT)
            if masked:
                key_at = c * CHUNK + lax.broadcasted_iota(jnp.int32, (CHUNK, width), 0)
                row_at = row_base + lax.rem(
                    lax.broadcasted_iota(jnp.int32, (CHUNK, width), 1), tokens
                )
                s = jnp.where(key_at <= row_at, s, masked_score)
            s_scr[rows, :width] = s
            return jnp.maximum(top, fold_rows(s, jnp.max))

        top = lax.fori_loop(
            0, last, lambda c, t: scores(c, t, False),
            jnp.full((8, width), masked_score, jnp.float32),
        )
        top = scores(last, top, True)
        shift = jnp.max(top, axis=0, keepdims=True) * to_exp2

        def weigh(c, carry):
            total, term = carry
            rows = rows_at(c)
            e = jnp.exp2(s_scr[rows, :width] * to_exp2 - shift)
            dp = matmul(kv_ref[rows, HD:], do, NT)
            s_scr[rows, :width] = e
            dp_scr[rows, :width] = dp
            return (total + fold_rows(e, jnp.sum), term + fold_rows(e * dp, jnp.sum))

        zero = jnp.zeros((8, width), jnp.float32)
        total, term = lax.fori_loop(0, last + 1, weigh, (zero, zero))
        inverse = 1.0 / jnp.sum(total, axis=0, keepdims=True)
        row_term = jnp.sum(term, axis=0, keepdims=True) * inverse

        def grads(c, dqt):
            rows = rows_at(c)
            p = s_scr[rows, :width] * inverse
            ds = (p * (dp_scr[rows, :width] - row_term)).astype(jnp.bfloat16)
            acc[rows, HD:] += matmul(p.astype(jnp.bfloat16), do, NN)
            acc[rows, :HD] += matmul(ds, q, NN)
            return dqt + matmul(kt_scr[:, rows], ds, NN)

        dqt = lax.fori_loop(0, last + 1, grads, jnp.zeros((HD, width), jnp.float32))
        dq = ((dqt * scaling).T).astype(dq_ref.dtype)
        for i in range(count):
            columns = pl.ds(pl.multiple_of((head + i) * HD, HD), HD)
            dq_ref[:, columns] = dq[i * tokens:(i + 1) * tokens, :]

    def pair(i, _):
        run_heads(first_head + 2 * i, 2)
        return 0

    lax.fori_loop(0, head_count // 2, pair, 0)

    @pl.when(head_count % 2 == 1)
    def _():
        run_heads(first_head + head_count - 1, 1)

    def finish(c, _):
        rows = rows_at(c)
        dkv_ref[rows, :HD] = (acc[rows, :HD] * scaling).astype(dkv_ref.dtype)
        dkv_ref[rows, HD:] = acc[rows, HD:].astype(dkv_ref.dtype)
        return 0

    lax.fori_loop(0, last + 1, finish, 0)

    def clear(c, _):
        dkv_ref[rows_at(c), :] = jnp.zeros((CHUNK, 2 * HD), dkv_ref.dtype)
        return 0

    lax.fori_loop(last + 1, dkv_ref.shape[0] // CHUNK, clear, 0)


def attention_grads(queries, grads, kv, info):
    tokens, width = queries.shape
    sequence = kv.shape[0]
    whole = pl.BlockSpec((tokens, width), lambda g, info: (0, 0))
    group_block = pl.BlockSpec((sequence, 2 * HD), lambda g, info: (0, g))
    return pl.pallas_call(
        attention_kernel,
        out_shape=(
            jax.ShapeDtypeStruct((tokens, width), jnp.bfloat16),
            jax.ShapeDtypeStruct(kv.shape, jnp.bfloat16),
        ),
        grid_spec=pltpu.PrefetchScalarGridSpec(
            num_scalar_prefetch=1,
            grid=(KVG,),
            in_specs=[whole, whole, group_block],
            out_specs=[whole, group_block],
            scratch_shapes=[
                pltpu.VMEM((2 * tokens, HD), jnp.bfloat16),
                pltpu.VMEM((2 * tokens, HD), jnp.bfloat16),
                pltpu.VMEM((sequence, 2 * tokens), jnp.float32),
                pltpu.VMEM((sequence, 2 * tokens), jnp.float32),
                pltpu.VMEM((sequence, 2 * HD), jnp.float32),
                pltpu.VMEM((HD, sequence), jnp.bfloat16),
            ],
        ),
        compiler_params=pltpu.CompilerParams(
            dimension_semantics=("arbitrary",), vmem_limit_bytes=48 * 1024 * 1024
        ),
        cost_estimate=pl.CostEstimate(
            flops=2 * 5 * HKEPT * tokens * sequence * HD,
            bytes_accessed=30 * 1024 * 1024,
            transcendentals=HKEPT * tokens * sequence,
        ),
        name="attention_grads",
    )(info, queries, grads, kv)


def local(query_states, key_states, value_states, output_grad, layer_input, head_counts):
    tokens = query_states.shape[1]
    input_parts = lax.all_to_all(
        layer_input, "dp", split_axis=2, concat_axis=0, tiled=True
    )
    keys = key_states[0].reshape(tokens, KVG, 1, HD)
    values = value_states[0].reshape(tokens, KVG, 1, HD)
    kv_local = jnp.concatenate([keys, values], axis=2).reshape(tokens, 2 * KVG * HD)
    kv = lax.all_gather(kv_local, "seq", axis=0, tiled=True)
    group_ends = jnp.cumsum(head_counts)
    info = jnp.concatenate(
        [group_ends - head_counts, head_counts, lax.axis_index("seq").reshape(1)]
    ).astype(jnp.int32)
    query_grad, dkv = attention_grads(query_states[0], output_grad[0], kv, info)
    summed = lax.psum_scatter(dkv, "seq", scatter_dimension=0, tiled=True)
    summed = summed.reshape(tokens, KVG, 2, HD)
    key_grad = summed[:, :, 0, :].reshape(1, tokens, KVG * HD)
    value_window = summed[:, :VGW, 1, :].reshape(1, tokens, VGW * HD)
    value_all = lax.all_gather(value_window, "dp", axis=0, tiled=True)
    weight_part = lax.dot_general(
        input_parts.reshape(-1, input_parts.shape[2]),
        value_all.reshape(-1, VGW * HD),
        (((0,), (0,)), ((), ())),
        preferred_element_type=jnp.float32,
    )
    weight_grad = lax.psum_scatter(weight_part, "seq", scatter_dimension=0, tiled=True)
    return (query_grad[None], key_grad, weight_grad)


def solution(mesh):
    placed = P("dp", "seq", None)
    return jax.shard_map(
        local,
        mesh=mesh,
        in_specs=(placed, placed, placed, placed, placed, P()),
        out_specs=(placed, placed, P(("dp", "seq"), None)),
        check_vma=False,
    )
```

```python
import functools
import math

import jax
import jax.numpy as jnp
from jax import lax
from jax.experimental import pallas as pl
from jax.experimental.pallas import tpu as pltpu
from jax.sharding import PartitionSpec as P

HD = 128
KVG = 8
HKEPT = 40
VGW = 4
CHUNK = 512

masked_score = -1e30
NT = (((1,), (1,)), ((), ()))
NN = (((1,), (0,)), ((), ()))


def matmul(a, b, dims):
    return lax.dot_general(a, b, dims, preferred_element_type=jnp.float32)


def fold_rows(x, op):
    rows, columns = x.shape
    return op(x.reshape(rows // 8, 8, columns), axis=0)


MESH = pl.DeviceIdType.MESH


def barrier_with(peers):
    barrier = pltpu.get_barrier_semaphore()
    for peer in peers:
        pl.semaphore_signal(barrier, inc=1, device_id=peer, device_id_type=MESH)
    pl.semaphore_wait(barrier, len(peers))


class Sender:
    def __init__(self, send_sems, recv_sems):
        self.send_sems, self.recv_sems, self.used = send_sems, recv_sems, 0

    def start(self, source, target, peer):
        copy = pltpu.make_async_remote_copy(
            src_ref=source,
            dst_ref=target,
            send_sem=self.send_sems.at[self.used],
            recv_sem=self.recv_sems.at[self.used],
            device_id=peer,
            device_id_type=MESH,
        )
        self.used += 1
        copy.start()
        return copy


def places():
    dp = lax.axis_index("dp")
    seq = lax.axis_index("seq")
    dps = lax.axis_size("dp")
    chips = lax.axis_size("seq") // 2
    z = seq // 2
    core = lax.rem(seq, 2)
    partner = (dp, 2 * z + 1 - core)

    def chip(offset):
        return (dp, 2 * lax.rem(z + offset + chips, chips) + core)

    def row(offset):
        return (lax.rem(dp + offset, dps), seq)

    return dp, seq, dps, chips, z, core, partner, chip, row


def gather_kernel(k_ref, v_ref, x_ref, kv_out, x_out, sends, recvs, local_sems):
    dp, seq, dps, chips, z, core, partner, chip, row = places()
    half = chips // 2
    width = k_ref.shape[1]
    parts = x_out.shape[2]
    barrier_with(
        [chip(1), chip(-1), partner] + [row(k) for k in range(1, dps)]
    )
    sender = Sender(sends, recvs)
    mine = kv_out.at[seq]
    key_part, value_part = pl.ds(0, width), pl.ds(width, width)
    first = {}
    for way in (1, -1):
        first[way] = [
            sender.start(k_ref, mine.at[:, key_part], chip(way)),
            sender.start(v_ref, mine.at[:, value_part], chip(way)),
        ]
    passed = [
        sender.start(k_ref, mine.at[:, key_part], partner),
        sender.start(v_ref, mine.at[:, value_part], partner),
    ]
    locals_ = [
        pltpu.make_async_copy(k_ref, mine.at[:, key_part], local_sems.at[0]),
        pltpu.make_async_copy(v_ref, mine.at[:, value_part], local_sems.at[1]),
        pltpu.make_async_copy(
            x_ref.at[:, pl.ds(pl.multiple_of(dp * parts, parts), parts)],
            x_out.at[dp], local_sems.at[2],
        ),
    ]
    for copy in locals_:
        copy.start()
    exchanged = []
    for k in range(1, dps):
        target = lax.rem(dp + k, dps)
        exchanged.append(
            sender.start(
                x_ref.at[:, pl.ds(pl.multiple_of(target * parts, parts), parts)],
                x_out.at[dp], row(k),
            )
        )
    waiting = dict(first)
    sent = []
    for step in range(1, half + 1):
        for way in (1, -1):
            for copy in waiting[way]:
                copy.wait_recv()
            sent += waiting[way]
            slot = 2 * lax.rem(z - way * step + chips, chips) + core
            block = kv_out.at[slot]
            if step == half:
                part = pl.ds(0 if way == 1 else width, width)
                block = block.at[:, part]
                passed.append(sender.start(block, block, partner))
                continue
            onward = block
            if step == half - 1:
                part = pl.ds(0 if way == 1 else width, width)
                onward = block.at[:, part]
            waiting[way] = [sender.start(onward, onward, chip(way))]
            passed.append(sender.start(block, block, partner))
    for copy in locals_:
        copy.wait()
    for copy in passed + exchanged:
        copy.wait_recv()
    for copy in sent + passed + exchanged:
        copy.wait_send()


def gather_exchange(keys, values, layer_input, first_columns):
    tokens = keys.shape[0]
    dps = lax.axis_size("dp")
    members = lax.axis_size("seq")
    chips = members // 2
    width = VGW * HD
    parts = layer_input.shape[1] // dps
    copies = 4 + 2 + (dps - 1) + 2 * (chips // 2 - 1) + 2 * (chips // 2)
    column = pl.BlockSpec((tokens, width), lambda i: (0, 0))
    return pl.pallas_call(
        gather_kernel,
        out_shape=(
            jax.ShapeDtypeStruct((members, tokens, 2 * width), jnp.bfloat16),
            jax.ShapeDtypeStruct((dps, tokens, parts), jnp.bfloat16),
        ),
        grid=(1,),
        in_specs=[column, column, pl.BlockSpec(memory_space=pltpu.VMEM)],
        out_specs=(pl.BlockSpec(memory_space=pl.ANY), pl.BlockSpec(memory_space=pl.ANY)),
        scratch_shapes=[
            pltpu.SemaphoreType.DMA((copies,)),
            pltpu.SemaphoreType.DMA((copies,)),
            pltpu.SemaphoreType.DMA((3,)),
        ],
        compiler_params=pltpu.CompilerParams(collective_id=0, has_side_effects=True),
        name="gather_exchange",
    )(keys, values, layer_input)


def reduce_kernel(
    dk_ref, v_ref, x_ref, dk_out, w_out,
    pair_k, ring_in, ring_out, fin_out, fin_in,
    v_all, w_part, w_pair, w_sum, w_in, w_fin, w_fin_in,
    sends, recvs, local_sem,
):
    dp, seq, dps, chips, z, core, partner, chip, row = places()
    tokens = v_ref.shape[0]
    half = dk_ref.shape[2] // 2
    quarter = half // 2
    whalf = w_part.shape[2] // 2
    other = 1 - core
    barrier_with(
        [partner]
        + [chip(k) for k in range(1, chips)]
        + [row(k) for k in range(1, dps)]
    )
    sender = Sender(sends, recvs)

    def at_chip(offset):
        return lax.rem(z + offset + 2 * chips, chips)

    order = []
    for k in range(1, chips // 2):
        order += [-k, k]
    order += [chips // 2, 0]
    index_of = {offset % chips: i for i, offset in enumerate(order)}
    mine_columns = pl.multiple_of(core * half, half)
    other_columns = pl.multiple_of(other * half, half)
    paired = [
        sender.start(
            dk_ref.at[at_chip(offset), :, pl.ds(other_columns, half)],
            pair_k.at[i], partner,
        )
        for i, offset in enumerate(order)
    ]
    own_v = pltpu.make_async_copy(v_ref, v_all.at[dp], local_sem.at[0])
    own_v.start()
    spread = [sender.start(v_ref, v_all.at[dp], row(k)) for k in range(1, dps)]

    arrived = set()

    def own_sum(offset, way_index, rows):
        i = index_of[offset % chips]
        if i not in arrived:
            paired[i].wait_recv()
            arrived.add(i)
        start = pl.multiple_of(mine_columns + way_index * quarter, quarter)
        mine = dk_ref[at_chip(offset), rows, pl.ds(start, quarter)]
        theirs = pair_k[i, rows, way_index * quarter:(way_index + 1) * quarter]
        return mine.astype(jnp.float32) + theirs.astype(jnp.float32)

    flights = {}
    sent = []
    for step in range(chips):
        for part in range(2):
            rows = slice(part * tokens, (part + 1) * tokens)
            for way_index, way in enumerate((1, -1)):
                value = own_sum(-way * (1 + step), way_index, rows)
                if step:
                    copy = flights[part, way]
                    copy.wait_recv()
                    sent.append(copy)
                    value = value + ring_in[way_index, part, step - 1].astype(jnp.float32)
                value = value.astype(jnp.bfloat16)
                if step < chips - 1:
                    ring_out[way_index, part, step] = value
                    flights[part, way] = sender.start(
                        ring_out.at[way_index, part, step],
                        ring_in.at[way_index, part, step],
                        chip(way),
                    )
                else:
                    fin_out[part, :, way_index * quarter:(way_index + 1) * quarter] = value
    back = sender.start(fin_out.at[other], fin_in, partner)
    dk_out[:, pl.ds(mine_columns, half)] = fin_out[core]

    own_v.wait()
    for copy in spread:
        copy.wait_recv()
    parts = x_ref.shape[2]
    joined = min(4, dps)

    def multiply(i, total):
        window = pl.ds(i * joined, joined)
        return total + lax.dot_general(
            x_ref[window].reshape(joined * tokens, parts),
            v_all[window].reshape(joined * tokens, v_ref.shape[1]),
            (((0,), (0,)), ((), ())),
            preferred_element_type=jnp.float32,
        )

    total = lax.fori_loop(
        0, dps // joined, multiply, jnp.zeros((parts, v_ref.shape[1]), jnp.float32)
    )
    w_part[...] = total.reshape(w_part.shape)
    w_mine = pl.multiple_of(core * whalf, whalf)
    w_other = pl.multiple_of(other * whalf, whalf)
    w_paired = sender.start(w_part.at[:, :, pl.ds(w_other, whalf)], w_pair, partner)
    back.wait_recv()
    dk_out[:, pl.ds(other_columns, half)] = fin_in[...]
    w_paired.wait_recv()
    w_sum[...] = w_part[:, :, pl.ds(w_mine, whalf)] + w_pair[...]
    direct = [
        sender.start(w_sum.at[at_chip(k)], w_in.at[k - 1], chip(k)) for k in range(1, chips)
    ]
    total = w_sum[z]
    for k, copy in enumerate(direct):
        copy.wait_recv()
        total = total + w_in[k]
    owned = w_out.shape[0]
    w_fin[...] = total.reshape(w_fin.shape)
    w_back = sender.start(w_fin.at[other], w_fin_in, partner)
    w_out[:, pl.ds(w_mine, whalf)] = w_fin[core]
    w_back.wait_recv()
    w_out[:, pl.ds(w_other, whalf)] = w_fin_in[...]
    for copy in paired + spread + sent + [back, w_paired, w_back] + direct:
        copy.wait_send()


def reduce_exchange(dk, value_window, input_parts):
    tokens, vwidth = value_window.shape
    dps = lax.axis_size("dp")
    members = lax.axis_size("seq")
    chips = members // 2
    kwidth = dk.shape[1]
    parts = input_parts.shape[2]
    owned = parts // members
    copies = chips + (dps - 1) + 4 * (chips - 1) + 3 + (chips - 1)
    vmem = pl.BlockSpec(memory_space=pltpu.VMEM)
    bf, f32 = jnp.bfloat16, jnp.float32
    return pl.pallas_call(
        reduce_kernel,
        out_shape=(
            jax.ShapeDtypeStruct((tokens, kwidth), bf),
            jax.ShapeDtypeStruct((owned, vwidth), f32),
        ),
        in_specs=[vmem] * 3,
        out_specs=(vmem, vmem),
        scratch_shapes=[
            pltpu.VMEM((chips, 2 * tokens, kwidth // 2), bf),
            pltpu.VMEM((2, 2, chips - 1, tokens, kwidth // 4), bf),
            pltpu.VMEM((2, 2, chips - 1, tokens, kwidth // 4), bf),
            pltpu.VMEM((2, tokens, kwidth // 2), bf),
            pltpu.VMEM((tokens, kwidth // 2), bf),
            pltpu.VMEM((dps, tokens, vwidth), bf),
            pltpu.VMEM((chips, 2 * owned, vwidth), f32),
            pltpu.VMEM((chips, 2 * owned, vwidth // 2), f32),
            pltpu.VMEM((chips, 2 * owned, vwidth // 2), f32),
            pltpu.VMEM((chips - 1, 2 * owned, vwidth // 2), f32),
            pltpu.VMEM((2, owned, vwidth // 2), f32),
            pltpu.VMEM((owned, vwidth // 2), f32),
            pltpu.SemaphoreType.DMA((copies,)),
            pltpu.SemaphoreType.DMA((copies,)),
            pltpu.SemaphoreType.DMA((1,)),
        ],
        compiler_params=pltpu.CompilerParams(
            collective_id=1, has_side_effects=True, vmem_limit_bytes=48 * 1024 * 1024
        ),
        name="reduce_exchange",
    )(dk.reshape(chips, 2 * tokens, kwidth), value_window, input_parts)


def attention_kernel(
    base, with_value, info, q_ref, do_ref, k_ref, v_ref, *refs
):
    if base:
        dq_before, *refs = refs
    dq_ref, dkv_ref, qs, dos, s_scr, dp_scr, acc, kt_scr = refs
    if base:
        @pl.when(pl.program_id(0) == 0)
        def _():
            dq_ref[...] = dq_before[...]

    group = base + pl.program_id(0)
    block = info[2 * KVG]
    first_head = info[group]
    head_count = info[KVG + group]
    tokens = q_ref.shape[0]
    scaling = 1.0 / math.sqrt(HD)
    to_exp2 = scaling * math.log2(math.e)
    last = (block * tokens) // CHUNK
    row_base = block * tokens

    def rows_at(c):
        return pl.ds(pl.multiple_of(c * CHUNK, CHUNK), CHUNK)

    def prepare(c, _):
        rows = rows_at(c)
        kt_scr[:, rows] = k_ref[rows, :].T
        acc[rows, :] = jnp.zeros((CHUNK, acc.shape[1]), jnp.float32)
        return 0

    lax.fori_loop(0, last + 1, prepare, 0)

    def run_heads(head, count):
        width = count * tokens
        for i in range(count):
            columns = pl.ds(pl.multiple_of((head + i) * HD, HD), HD)
            qs[i * tokens:(i + 1) * tokens, :] = q_ref[:, columns]
            dos[i * tokens:(i + 1) * tokens, :] = do_ref[:, columns]
        q = qs[:width, :]
        do = dos[:width, :]

        def scores(c, top, masked):
            rows = rows_at(c)
            s = matmul(k_ref[rows, :], q, NT)
            if masked:
                key_at = c * CHUNK + lax.broadcasted_iota(jnp.int32, (CHUNK, width), 0)
                row_at = row_base + lax.rem(
                    lax.broadcasted_iota(jnp.int32, (CHUNK, width), 1), tokens
                )
                s = jnp.where(key_at <= row_at, s, masked_score)
            s_scr[rows, :width] = s
            return jnp.maximum(top, fold_rows(s, jnp.max))

        top = lax.fori_loop(
            0, last, lambda c, t: scores(c, t, False),
            jnp.full((8, width), masked_score, jnp.float32),
        )
        top = scores(last, top, True)
        shift = jnp.max(top, axis=0, keepdims=True) * to_exp2

        def weigh(c, carry):
            total, term = carry
            rows = rows_at(c)
            e = jnp.exp2(s_scr[rows, :width] * to_exp2 - shift)
            dp = matmul(v_ref[rows, :], do, NT)
            s_scr[rows, :width] = e
            dp_scr[rows, :width] = dp
            return (total + fold_rows(e, jnp.sum), term + fold_rows(e * dp, jnp.sum))

        zero = jnp.zeros((8, width), jnp.float32)
        total, term = lax.fori_loop(0, last + 1, weigh, (zero, zero))
        inverse = 1.0 / jnp.sum(total, axis=0, keepdims=True)
        row_term = jnp.sum(term, axis=0, keepdims=True) * inverse

        def grads(c, dqt):
            rows = rows_at(c)
            p = s_scr[rows, :width] * inverse
            ds = (p * (dp_scr[rows, :width] - row_term)).astype(jnp.bfloat16)
            if with_value:
                acc[rows, HD:] += matmul(p.astype(jnp.bfloat16), do, NN)
            acc[rows, :HD] += matmul(ds, q, NN)
            return dqt + matmul(kt_scr[:, rows], ds, NN)

        dqt = lax.fori_loop(0, last + 1, grads, jnp.zeros((HD, width), jnp.float32))
        dq = ((dqt * scaling).T).astype(dq_ref.dtype)
        for i in range(count):
            columns = pl.ds(pl.multiple_of((head + i) * HD, HD), HD)
            dq_ref[:, columns] = dq[i * tokens:(i + 1) * tokens, :]

    def pair(i, _):
        run_heads(first_head + 2 * i, 2)
        return 0

    lax.fori_loop(0, head_count // 2, pair, 0)

    @pl.when(head_count % 2 == 1)
    def _():
        run_heads(first_head + head_count - 1, 1)

    def finish(c, _):
        rows = rows_at(c)
        dkv_ref[rows, :HD] = (acc[rows, :HD] * scaling).astype(dkv_ref.dtype)
        if with_value:
            dkv_ref[rows, HD:] = acc[rows, HD:].astype(dkv_ref.dtype)
        return 0

    lax.fori_loop(0, last + 1, finish, 0)

    def clear(c, _):
        dkv_ref[rows_at(c), :] = jnp.zeros((CHUNK, dkv_ref.shape[1]), dkv_ref.dtype)
        return 0

    lax.fori_loop(last + 1, dkv_ref.shape[0] // CHUNK, clear, 0)


def attention_grads(queries, grads, kv, info, base, with_value, before=None):
    tokens, width = queries.shape
    sequence, kv_width = kv.shape
    groups = kv_width // (2 * HD)
    wide = 2 * HD if with_value else HD
    whole = pl.BlockSpec((tokens, width), lambda g, info: (0, 0))
    key_block = pl.BlockSpec((sequence, HD), lambda g, info: (0, g))
    value_block = pl.BlockSpec((sequence, HD), lambda g, info: (0, groups + g))
    given = () if before is None else (before,)
    return pl.pallas_call(
        functools.partial(attention_kernel, base, with_value),
        out_shape=(
            jax.ShapeDtypeStruct((tokens, width), jnp.bfloat16),
            jax.ShapeDtypeStruct((sequence, groups * wide), jnp.bfloat16),
        ),
        grid_spec=pltpu.PrefetchScalarGridSpec(
            num_scalar_prefetch=1,
            grid=(groups,),
            in_specs=[whole, whole, key_block, value_block] + [whole] * len(given),
            out_specs=[whole, pl.BlockSpec((sequence, wide), lambda g, info: (0, g))],
            scratch_shapes=[
                pltpu.VMEM((2 * tokens, HD), jnp.bfloat16),
                pltpu.VMEM((2 * tokens, HD), jnp.bfloat16),
                pltpu.VMEM((sequence, 2 * tokens), jnp.float32),
                pltpu.VMEM((sequence, 2 * tokens), jnp.float32),
                pltpu.VMEM((sequence, wide), jnp.float32),
                pltpu.VMEM((HD, sequence), jnp.bfloat16),
            ],
        ),
        compiler_params=pltpu.CompilerParams(
            dimension_semantics=("arbitrary",), vmem_limit_bytes=48 * 1024 * 1024
        ),
        cost_estimate=pl.CostEstimate(
            flops=2 * 5 * HKEPT * tokens * sequence * HD,
            bytes_accessed=30 * 1024 * 1024,
            transcendentals=HKEPT * tokens * sequence,
        ),
        name="attention_grads",
    )(info, queries, grads, kv, kv, *given)


def local(query_states, key_states, value_states, output_grad, layer_input, head_counts):
    tokens = query_states.shape[1]
    keys, values, queries, grads = key_states[0], value_states[0], query_states[0], output_grad[0]
    split = VGW * HD
    group_ends = jnp.cumsum(head_counts)
    info = jnp.concatenate(
        [group_ends - head_counts, head_counts, lax.axis_index("seq").reshape(1)]
    ).astype(jnp.int32)
    kv_late = jnp.concatenate([keys[:, split:], values[:, split:]], axis=1)
    kv_first, input_parts = gather_exchange(keys, values, layer_input[0], split)
    kv_first, kv_late = lax.optimization_barrier((kv_first, kv_late))
    kv_first = kv_first.reshape(-1, 2 * split)
    kv_late = lax.all_gather(kv_late, "seq", axis=0, tiled=True)
    query_grad, dkv_first = attention_grads(queries, grads, kv_first, info, 0, True)
    query_grad, dk_late = attention_grads(
        queries, grads, kv_late, info, VGW, False, query_grad
    )
    summed = lax.psum_scatter(dkv_first, "seq", scatter_dimension=0, tiled=True)
    summed = summed.reshape(tokens, VGW, 2, HD)
    key_first = summed[:, :, 0, :].reshape(tokens, split)
    value_window = summed[:, :, 1, :].reshape(tokens, split)
    key_late, weight_grad = reduce_exchange(dk_late, value_window, input_parts)
    key_grad = jnp.concatenate([key_first, key_late], axis=1)
    return (query_grad[None], key_grad[None], weight_grad)


def solution(mesh):
    placed = P("dp", "seq", None)
    return jax.shard_map(
        local,
        mesh=mesh,
        in_specs=(placed, placed, placed, placed, placed, P()),
        out_specs=(placed, placed, P(("dp", "seq"), None)),
        check_vma=False,
    )
```

```python
import functools
import math

import jax
import jax.numpy as jnp
from jax import lax
from jax.experimental import pallas as pl
from jax.experimental.pallas import tpu as pltpu
from jax.sharding import PartitionSpec as P

HD = 128
KVG = 8
HKEPT = 40
VGW = 4
CHUNK = 512

masked_score = -1e30
NT = (((1,), (1,)), ((), ()))
NN = (((1,), (0,)), ((), ()))


def matmul(a, b, dims):
    return lax.dot_general(a, b, dims, preferred_element_type=jnp.float32)


def fold_rows(x, op):
    rows, columns = x.shape
    return op(x.reshape(rows // 8, 8, columns), axis=0)


MESH = pl.DeviceIdType.MESH


def barrier_with(peers):
    barrier = pltpu.get_barrier_semaphore()
    for peer in peers:
        pl.semaphore_signal(barrier, inc=1, device_id=peer, device_id_type=MESH)
    pl.semaphore_wait(barrier, len(peers))


class Sender:
    def __init__(self, send_sems, recv_sems):
        self.send_sems, self.recv_sems, self.used = send_sems, recv_sems, 0

    def start(self, source, target, peer):
        copy = pltpu.make_async_remote_copy(
            src_ref=source,
            dst_ref=target,
            send_sem=self.send_sems.at[self.used],
            recv_sem=self.recv_sems.at[self.used],
            device_id=peer,
            device_id_type=MESH,
        )
        self.used += 1
        copy.start()
        return copy


def places():
    dp = lax.axis_index("dp")
    seq = lax.axis_index("seq")
    dps = lax.axis_size("dp")
    chips = lax.axis_size("seq") // 2
    z = seq // 2
    core = lax.rem(seq, 2)
    partner = (dp, 2 * z + 1 - core)

    def chip(offset):
        return (dp, 2 * lax.rem(z + offset + chips, chips) + core)

    def row(offset):
        return (lax.rem(dp + offset, dps), seq)

    return dp, seq, dps, chips, z, core, partner, chip, row


def gather_kernel(k_ref, v_ref, x_ref, kv_out, x_out, sends, recvs, local_sems):
    dp, seq, dps, chips, z, core, partner, chip, row = places()
    half = chips // 2
    width = k_ref.shape[1]
    parts = x_out.shape[2]
    barrier_with(
        [chip(1), chip(-1), partner] + [row(k) for k in range(1, dps)]
    )
    sender = Sender(sends, recvs)
    spans = (pl.ds(0, width), pl.ds(width, width))
    sources = (k_ref, v_ref)
    mine = kv_out.at[seq]
    flights = {}
    for part in range(2):
        for way in (1, -1):
            flights[part, way] = sender.start(
                sources[part], mine.at[:, spans[part]], chip(way)
            )
    passed = [
        sender.start(sources[part], mine.at[:, spans[part]], partner) for part in range(2)
    ]
    locals_ = [
        pltpu.make_async_copy(sources[part], mine.at[:, spans[part]], local_sems.at[part])
        for part in range(2)
    ] + [
        pltpu.make_async_copy(
            x_ref.at[:, pl.ds(pl.multiple_of(dp * parts, parts), parts)],
            x_out.at[dp], local_sems.at[2],
        ),
    ]
    for copy in locals_:
        copy.start()
    exchanged = []
    for k in range(1, dps):
        target = lax.rem(dp + k, dps)
        exchanged.append(
            sender.start(
                x_ref.at[:, pl.ds(pl.multiple_of(target * parts, parts), parts)],
                x_out.at[dp], row(k),
            )
        )
    sent = []
    for step in range(1, half + 1):
        for part in range(2):
            for way in (1, -1):
                last_way = 1 if part == 0 else -1
                if step == half and way != last_way:
                    continue
                copy = flights[part, way]
                copy.wait_recv()
                sent.append(copy)
                slot = 2 * lax.rem(z - way * step + chips, chips) + core
                block = kv_out.at[slot, :, spans[part]]
                if step < half - 1 or (step == half - 1 and way == last_way):
                    flights[part, way] = sender.start(block, block, chip(way))
                passed.append(sender.start(block, block, partner))
    for copy in locals_:
        copy.wait()
    for copy in passed + exchanged:
        copy.wait_recv()
    for copy in sent + passed + exchanged:
        copy.wait_send()


def gather_exchange(keys, values, layer_input):
    tokens, width = keys.shape
    dps = lax.axis_size("dp")
    members = lax.axis_size("seq")
    chips = members // 2
    parts = layer_input.shape[1] // dps
    copies = 4 * (chips // 2) + 4 * (chips // 2) + dps
    vmem = pl.BlockSpec(memory_space=pltpu.VMEM)
    return pl.pallas_call(
        gather_kernel,
        out_shape=(
            jax.ShapeDtypeStruct((members, tokens, 2 * width), jnp.bfloat16),
            jax.ShapeDtypeStruct((dps, tokens, parts), jnp.bfloat16),
        ),
        in_specs=[vmem] * 3,
        out_specs=(pl.BlockSpec(memory_space=pl.ANY), pl.BlockSpec(memory_space=pl.ANY)),
        scratch_shapes=[
            pltpu.SemaphoreType.DMA((copies,)),
            pltpu.SemaphoreType.DMA((copies,)),
            pltpu.SemaphoreType.DMA((3,)),
        ],
        compiler_params=pltpu.CompilerParams(collective_id=0, has_side_effects=True),
        name="gather_exchange",
    )(keys, values, layer_input)


class Ring:
    def __init__(self, sender, partial, pair_in, ring_in, ring_out, fin_out):
        self.sender, self.partial, self.pair_in = sender, partial, pair_in
        self.ring_in, self.ring_out, self.fin_out = ring_in, ring_out, fin_out
        _, _, _, self.chips, self.z, self.core, self.partner, self.chip, _ = places()
        self.half = pair_in.shape[2]
        self.quarter = self.half // 2
        self.tokens = fin_out.shape[1]
        self.flights, self.sent, self.arrived = {}, [], set()
        order = []
        for k in range(1, self.chips // 2):
            order += [-k, k]
        order += [self.chips // 2, 0]
        self.index_of = {offset % self.chips: i for i, offset in enumerate(order)}
        theirs = pl.ds(pl.multiple_of((1 - self.core) * self.half, self.half), self.half)
        self.paired = [
            sender.start(
                partial.at[self.at_chip(offset), :, theirs], pair_in.at[i], self.partner
            )
            for i, offset in enumerate(order)
        ]

    def at_chip(self, offset):
        return lax.rem(self.z + offset + 2 * self.chips, self.chips)

    def own_sum(self, offset, way_index, rows):
        i = self.index_of[offset % self.chips]
        if i not in self.arrived:
            self.paired[i].wait_recv()
            self.arrived.add(i)
        begin = way_index * self.quarter
        start = pl.multiple_of(self.core * self.half + begin, self.quarter)
        mine = self.partial[self.at_chip(offset), rows, pl.ds(start, self.quarter)]
        theirs = self.pair_in[i, rows, begin:begin + self.quarter]
        return mine.astype(jnp.float32) + theirs.astype(jnp.float32)

    def step(self, step):
        tokens = self.tokens
        for part in range(2):
            rows = slice(part * tokens, (part + 1) * tokens)
            for way_index, way in enumerate((1, -1)):
                value = self.own_sum(-way * (1 + step), way_index, rows)
                if step:
                    copy = self.flights[part, way]
                    copy.wait_recv()
                    self.sent.append(copy)
                    value = value + self.ring_in[way_index, part, step - 1].astype(jnp.float32)
                value = value.astype(jnp.bfloat16)
                if step < self.chips - 1:
                    self.ring_out[way_index, part, step] = value
                    self.flights[part, way] = self.sender.start(
                        self.ring_out.at[way_index, part, step],
                        self.ring_in.at[way_index, part, step],
                        self.chip(way),
                    )
                else:
                    begin = way_index * self.quarter
                    self.fin_out[part, :, begin:begin + self.quarter] = value

    def copies(self):
        return self.paired + self.sent


def reduce_kernel(
    dv_ref, dka_ref, dkb_ref, x_ref, dk_out, w_out,
    pairs, rings_in, rings_out, fins,
    v_all, w_part, w_pair, w_sum, w_in, w_fin, w_fin_in,
    sends, recvs, local_sem,
):
    dp, seq, dps, chips, z, core, partner, chip, row = places()
    tokens = fins.shape[2]
    width = dv_ref.shape[2]
    half = width // 2
    whalf = w_part.shape[2] // 2
    other = 1 - core
    barrier_with(
        [partner]
        + [chip(k) for k in range(1, chips)]
        + [row(k) for k in range(1, dps)]
    )
    sender = Sender(sends, recvs)
    value, key_a, key_b = [
        Ring(sender, ref, pairs.at[i], rings_in.at[i], rings_out.at[i], fins.at[i])
        for i, ref in enumerate((dv_ref, dka_ref, dkb_ref))
    ]
    mine_columns = pl.ds(pl.multiple_of(core * half, half), half)
    done = 0
    for step in range(chips):
        value.step(step)
        if step % 2 == 0 and done < chips - 5:
            key_a.step(done)
            key_b.step(done)
            done += 1
    v_mine = v_all.at[dp, :, mine_columns]
    kept = pltpu.make_async_copy(fins.at[0, core], v_mine, local_sem.at[0])
    kept.start()
    v_back = sender.start(fins.at[0, other], v_mine, partner)
    kept.wait()
    v_back.wait_recv()
    spread = [sender.start(v_all.at[dp], v_all.at[dp], row(k)) for k in range(1, dps)]
    for step in range(done, chips):
        key_a.step(step)
        key_b.step(step)
    k_kept, k_back = [], []
    for i in (1, 2):
        start = pl.multiple_of((i - 1) * width + core * half, half)
        target = dk_out.at[:, pl.ds(start, half)]
        k_kept.append(pltpu.make_async_copy(fins.at[i, core], target, local_sem.at[i]))
        k_kept[-1].start()
        k_back.append(sender.start(fins.at[i, other], target, partner))

    for copy in spread:
        copy.wait_recv()
    parts = x_ref.shape[2]
    joined = min(4, dps)

    def multiply(i, total):
        window = pl.ds(i * joined, joined)
        return total + lax.dot_general(
            x_ref[window].reshape(joined * tokens, parts),
            v_all[window].reshape(joined * tokens, width),
            (((0,), (0,)), ((), ())),
            preferred_element_type=jnp.float32,
        )

    total = lax.fori_loop(
        0, dps // joined, multiply, jnp.zeros((parts, width), jnp.float32)
    )
    w_part[...] = total.reshape(w_part.shape)
    w_mine = pl.multiple_of(core * whalf, whalf)
    w_other = pl.multiple_of(other * whalf, whalf)
    w_paired = sender.start(w_part.at[:, :, pl.ds(w_other, whalf)], w_pair, partner)
    for copy in k_kept:
        copy.wait()
    for copy in k_back:
        copy.wait_recv()
    w_paired.wait_recv()
    w_sum[...] = w_part[:, :, pl.ds(w_mine, whalf)] + w_pair[...]
    direct = [
        sender.start(w_sum.at[value.at_chip(k)], w_in.at[k - 1], chip(k))
        for k in range(1, chips)
    ]
    total = w_sum[z]
    for k, copy in enumerate(direct):
        copy.wait_recv()
        total = total + w_in[k]
    w_fin[...] = total.reshape(w_fin.shape)
    w_back = sender.start(w_fin.at[other], w_fin_in, partner)
    w_out[:, pl.ds(w_mine, whalf)] = w_fin[core]
    w_back.wait_recv()
    w_out[:, pl.ds(w_other, whalf)] = w_fin_in[...]
    copies = value.copies() + key_a.copies() + key_b.copies()
    for copy in copies + spread + direct + k_back + [v_back, w_paired, w_back]:
        copy.wait_send()


def reduce_exchange(dv, dka, dkb, input_parts):
    dps, tokens, parts = input_parts.shape
    members = lax.axis_size("seq")
    chips = members // 2
    width = dv.shape[1]
    owned = parts // members
    copies = 3 * (chips + 4 * (chips - 1)) + (dps - 1) + (chips - 1) + 5
    vmem = pl.BlockSpec(memory_space=pltpu.VMEM)
    bf, f32 = jnp.bfloat16, jnp.float32
    blocks = [x.reshape(chips, 2 * tokens, width) for x in (dv, dka, dkb)]
    return pl.pallas_call(
        reduce_kernel,
        out_shape=(
            jax.ShapeDtypeStruct((tokens, 2 * width), bf),
            jax.ShapeDtypeStruct((owned, width), f32),
        ),
        in_specs=[vmem] * 4,
        out_specs=(vmem, vmem),
        scratch_shapes=[
            pltpu.VMEM((3, chips, 2 * tokens, width // 2), bf),
            pltpu.VMEM((3, 2, 2, chips - 1, tokens, width // 4), bf),
            pltpu.VMEM((3, 2, 2, chips - 1, tokens, width // 4), bf),
            pltpu.VMEM((3, 2, tokens, width // 2), bf),
            pltpu.VMEM((dps, tokens, width), bf),
            pltpu.VMEM((chips, 2 * owned, width), f32),
            pltpu.VMEM((chips, 2 * owned, width // 2), f32),
            pltpu.VMEM((chips, 2 * owned, width // 2), f32),
            pltpu.VMEM((chips - 1, 2 * owned, width // 2), f32),
            pltpu.VMEM((2, owned, width // 2), f32),
            pltpu.VMEM((owned, width // 2), f32),
            pltpu.SemaphoreType.DMA((copies,)),
            pltpu.SemaphoreType.DMA((copies,)),
            pltpu.SemaphoreType.DMA((3,)),
        ],
        compiler_params=pltpu.CompilerParams(
            collective_id=1, has_side_effects=True, vmem_limit_bytes=48 * 1024 * 1024
        ),
        name="reduce_exchange",
    )(*blocks, input_parts)


def attention_kernel(
    base, with_value, info, q_ref, do_ref, k_ref, v_ref, *refs
):
    if base:
        dq_before, *refs = refs
    if with_value:
        dq_ref, dk_ref, dv_ref, *refs = refs
    else:
        dq_ref, dk_ref, *refs = refs
    qs, dos, s_scr, dp_scr, acc, kt_scr = refs
    if base:
        @pl.when(pl.program_id(0) == 0)
        def _():
            dq_ref[...] = dq_before[...]

    group = base + pl.program_id(0)
    block = info[2 * KVG]
    first_head = info[group]
    head_count = info[KVG + group]
    tokens = q_ref.shape[0]
    scaling = 1.0 / math.sqrt(HD)
    to_exp2 = scaling * math.log2(math.e)
    last = (block * tokens) // CHUNK
    row_base = block * tokens

    def rows_at(c):
        return pl.ds(pl.multiple_of(c * CHUNK, CHUNK), CHUNK)

    def prepare(c, _):
        rows = rows_at(c)
        kt_scr[:, rows] = k_ref[rows, :].T
        acc[rows, :] = jnp.zeros((CHUNK, acc.shape[1]), jnp.float32)
        return 0

    lax.fori_loop(0, last + 1, prepare, 0)

    def run_heads(head, count):
        width = count * tokens
        for i in range(count):
            columns = pl.ds(pl.multiple_of((head + i) * HD, HD), HD)
            qs[i * tokens:(i + 1) * tokens, :] = q_ref[:, columns]
            dos[i * tokens:(i + 1) * tokens, :] = do_ref[:, columns]
        q = qs[:width, :]
        do = dos[:width, :]

        def scores(c, top, masked):
            rows = rows_at(c)
            s = matmul(k_ref[rows, :], q, NT)
            if masked:
                key_at = c * CHUNK + lax.broadcasted_iota(jnp.int32, (CHUNK, width), 0)
                row_at = row_base + lax.rem(
                    lax.broadcasted_iota(jnp.int32, (CHUNK, width), 1), tokens
                )
                s = jnp.where(key_at <= row_at, s, masked_score)
            s_scr[rows, :width] = s
            return jnp.maximum(top, fold_rows(s, jnp.max))

        top = lax.fori_loop(
            0, last, lambda c, t: scores(c, t, False),
            jnp.full((8, width), masked_score, jnp.float32),
        )
        top = scores(last, top, True)
        shift = jnp.max(top, axis=0, keepdims=True) * to_exp2

        def weigh(c, carry):
            total, term = carry
            rows = rows_at(c)
            e = jnp.exp2(s_scr[rows, :width] * to_exp2 - shift)
            dp = matmul(v_ref[rows, :], do, NT)
            s_scr[rows, :width] = e
            dp_scr[rows, :width] = dp
            return (total + fold_rows(e, jnp.sum), term + fold_rows(e * dp, jnp.sum))

        zero = jnp.zeros((8, width), jnp.float32)
        total, term = lax.fori_loop(0, last + 1, weigh, (zero, zero))
        inverse = 1.0 / jnp.sum(total, axis=0, keepdims=True)
        row_term = jnp.sum(term, axis=0, keepdims=True) * inverse

        def grads(c, dqt):
            rows = rows_at(c)
            p = s_scr[rows, :width] * inverse
            ds = (p * (dp_scr[rows, :width] - row_term)).astype(jnp.bfloat16)
            if with_value:
                acc[rows, HD:] += matmul(p.astype(jnp.bfloat16), do, NN)
            acc[rows, :HD] += matmul(ds, q, NN)
            return dqt + matmul(kt_scr[:, rows], ds, NN)

        dqt = lax.fori_loop(0, last + 1, grads, jnp.zeros((HD, width), jnp.float32))
        dq = ((dqt * scaling).T).astype(dq_ref.dtype)
        for i in range(count):
            columns = pl.ds(pl.multiple_of((head + i) * HD, HD), HD)
            dq_ref[:, columns] = dq[i * tokens:(i + 1) * tokens, :]

    def pair(i, _):
        run_heads(first_head + 2 * i, 2)
        return 0

    lax.fori_loop(0, head_count // 2, pair, 0)

    @pl.when(head_count % 2 == 1)
    def _():
        run_heads(first_head + head_count - 1, 1)

    def finish(c, _):
        rows = rows_at(c)
        dk_ref[rows, :] = (acc[rows, :HD] * scaling).astype(dk_ref.dtype)
        if with_value:
            dv_ref[rows, :] = acc[rows, HD:].astype(dv_ref.dtype)
        return 0

    lax.fori_loop(0, last + 1, finish, 0)

    def clear(c, _):
        for ref in (dk_ref, dv_ref) if with_value else (dk_ref,):
            ref[rows_at(c), :] = jnp.zeros((CHUNK, HD), ref.dtype)
        return 0

    lax.fori_loop(last + 1, dk_ref.shape[0] // CHUNK, clear, 0)


def attention_grads(queries, grads, kv, info, base, with_value, before=None):
    tokens, width = queries.shape
    sequence, kv_width = kv.shape
    groups = VGW
    offset = kv_width // (2 * HD)
    wide = 2 * HD if with_value else HD
    whole = pl.BlockSpec((tokens, width), lambda g, info: (0, 0))
    key_block = pl.BlockSpec((sequence, HD), lambda g, info: (0, base + g))
    value_block = pl.BlockSpec((sequence, HD), lambda g, info: (0, offset + base + g))
    group_block = pl.BlockSpec((sequence, HD), lambda g, info: (0, g))
    given = () if before is None else (before,)
    return pl.pallas_call(
        functools.partial(attention_kernel, base, with_value),
        out_shape=(
            jax.ShapeDtypeStruct((tokens, width), jnp.bfloat16),
        ) + (jax.ShapeDtypeStruct((sequence, groups * HD), jnp.bfloat16),) * (wide // HD),
        grid_spec=pltpu.PrefetchScalarGridSpec(
            num_scalar_prefetch=1,
            grid=(groups,),
            in_specs=[whole, whole, key_block, value_block] + [whole] * len(given),
            out_specs=[whole] + [group_block] * (wide // HD),
            scratch_shapes=[
                pltpu.VMEM((2 * tokens, HD), jnp.bfloat16),
                pltpu.VMEM((2 * tokens, HD), jnp.bfloat16),
                pltpu.VMEM((sequence, 2 * tokens), jnp.float32),
                pltpu.VMEM((sequence, 2 * tokens), jnp.float32),
                pltpu.VMEM((sequence, wide), jnp.float32),
                pltpu.VMEM((HD, sequence), jnp.bfloat16),
            ],
        ),
        compiler_params=pltpu.CompilerParams(
            dimension_semantics=("arbitrary",), vmem_limit_bytes=48 * 1024 * 1024
        ),
        cost_estimate=pl.CostEstimate(
            flops=2 * 5 * HKEPT * tokens * sequence * HD,
            bytes_accessed=30 * 1024 * 1024,
            transcendentals=HKEPT * tokens * sequence,
        ),
        name="attention_grads",
    )(info, queries, grads, kv, kv, *given)


def local(query_states, key_states, value_states, output_grad, layer_input, head_counts):
    queries, grads = query_states[0], output_grad[0]
    group_ends = jnp.cumsum(head_counts)
    info = jnp.concatenate(
        [group_ends - head_counts, head_counts, lax.axis_index("seq").reshape(1)]
    ).astype(jnp.int32)
    kv, input_parts = gather_exchange(key_states[0], value_states[0], layer_input[0])
    kv = kv.reshape(-1, kv.shape[2])
    query_grad, dk_first, dv = attention_grads(queries, grads, kv, info, 0, True)
    query_grad, dk_late = attention_grads(queries, grads, kv, info, VGW, False, query_grad)
    key_grad, weight_grad = reduce_exchange(dv, dk_first, dk_late, input_parts)
    return (query_grad[None], key_grad[None], weight_grad)


def solution(mesh):
    placed = P("dp", "seq", None)
    return jax.shard_map(
        local,
        mesh=mesh,
        in_specs=(placed, placed, placed, placed, placed, P()),
        out_specs=(placed, placed, P(("dp", "seq"), None)),
        check_vma=False,
    )
```
